256 devices in a mesh: grp: 8 (over x, core), vocab: 32 (over y, z).
Axes of the slice: x: 4, y: 4, z: 8, core: 2. Of those that a mesh axis runs over, the one named last changes fastest.
Arguments:
- hidden: bfloat16 [1024, 16384], P('grp', 'vocab'), may hold values from -6 to 6
- flags: int32 [1024, 1], P('grp'), may hold values from 0 to 8; in each aligned block of 128 rows (0 to 127, 128 to 255, ...) at most 16 rows name the same one
- targets: int32 [1024], P('grp'), may hold values from 0 to 65535
- head: bfloat16 [16384, 65536], P('grp', 'vocab'), may hold values from -0.140625 to 0.140625
- lengths: int32 [8, 8], P('grp'), may hold values from 1 to 64, 128 in all within a row
Outputs:
- token_scores: float32 [1024], P('grp')
- doc_scores: float32 [8, 8], P('grp')
The draws below stay inside these ranges and needn't reach their ends.
Inputs may be any that keep to these rules, and one draw needn't show every extreme that they name: `flags`: A value below 8 names the scorer group of a scored row. Within the 128 rows of one shard no value occurs more than 16 times, and in every draw some value occurs exactly 16 times in some shard.
All inputs are finite; a program needn't handle non-finite values.
Results may differ from the reference program's by a relative error of at most 0.0003.
Values may be sent and summed in bfloat16 or wider, within the bound.
A program may use at most 128 MiB of HBM per device.

```python
import math
import jax
import jax.numpy as jnp
import numpy as np
from jax import lax

D = 16384
VOCAB = 65536
ROW_GRP = 128
DOCS = 8
SHARDS = 8
CAP = 16
ROWS = 1024


def head_columns(key, columns):
    base = jax.random.fold_in(key, 11)

    def one_column(column):
        return jax.random.truncated_normal(jax.random.fold_in(base, column), -6.0, 6.0, (D,), jnp.float32)
    return jax.vmap(one_column)(columns) * (3.0 / math.sqrt(D))


def draw_head(key, part):
    return head_columns(key, jnp.arange(VOCAB, dtype=jnp.int32)).T.astype(jnp.bfloat16)


def draw_hidden(key, part):
    key_one = jax.random.fold_in(jax.random.fold_in(key, 3), 0)
    return jax.random.truncated_normal(key_one, -6.0, 6.0, (ROWS, D), jnp.float32).astype(jnp.bfloat16)


def plant(values, stream_key, low, high):
    place = [jax.random.randint(jax.random.fold_in(stream_key, axis), (), 0, length) for axis, length in enumerate(values.shape)]
    main_axis = values.shape.index(max(values.shape))
    beside = place[:main_axis] + [(place[main_axis] + 1) % values.shape[main_axis]] + place[main_axis + 1:]
    return values.at[tuple(place)].set(low).at[tuple(beside)].set(high)


def cumulative_ranks(number_of, lean):
    portions = [(1 << 20) // math.isqrt(grade ** lean) + 1 for grade in range(1, number_of + 1)]
    deviation = 1 + sum(portions) // (1 << 30)
    return np.cumsum(np.array([max(1, weight // deviation) for weight in portions]))


def ranked_ids(key, extent, count, lean):
    grid = cumulative_ranks(count, lean)
    ticket = jax.random.randint(jax.random.fold_in(key, 1), extent, 0, int(grid[count - 1]))
    rank = jnp.searchsorted(jnp.asarray(grid, jnp.int32), ticket, side="right")
    return jax.random.permutation(jax.random.fold_in(key, 2), count)[rank].astype(jnp.int32)


def profile(count, total, bound, lean):
    loads = [(1 << 20) // math.isqrt(rank ** lean) + 1 for rank in range(2, count + 1)]
    surplus, given = total - bound - (count - 1), [1] * (count - 1)
    while surplus > 0:
        movable = [i for i in range(count - 1) if given[i] < bound]
        pool, budget = sum([loads[i] for i in movable]), surplus
        for i in movable:
            addition = min(bound - given[i], max(1, budget * loads[i] // pool), surplus)
            given[i] = given[i] + addition
            surplus = surplus - addition
    return np.array([bound] + given)


def uneven_parts(key, number_of, total, bound, skew):
    if number_of == 2:
        one = jax.random.randint(key, (), max(1, total - bound), min(bound, total - 1) + 1)
        return jnp.stack([one, total - one])
    sizes = jnp.asarray(profile(number_of, total, bound, skew), jnp.int32)
    twos = (number_of - 1) // 2
    giver, sink = sizes[1:1 + 2 * twos:2], sizes[2:2 + 2 * twos:2]
    room = jnp.minimum(giver - 1, bound - sink)
    passed = jax.random.randint(jax.random.fold_in(key, 1), (twos,), 0, 1 << 20) % (room + 1)
    sizes = sizes.at[1:1 + 2 * twos:2].set(giver - passed).at[2:2 + 2 * twos:2].set(sink + passed)
    return sizes[jax.random.permutation(jax.random.fold_in(key, 2), number_of)]


def shared_out(key, own, number, rows, count, top, most, lean):
    sequence = jax.random.permutation(key, count)
    heavy_load, common = shares(count, rows * top, most, lean, True), shares(count, rows * top, most, lean, False)
    places = jnp.arange(count)

    def named(sizes, turn):
        used = int((sizes > 0).sum())
        fixed = max(1, used // 4)
        passed = fixed + (places - fixed + turn * (used - fixed)) % max(1, count - fixed)
        return jnp.zeros((count,), jnp.int32).at[sequence[jnp.where(places < fixed, places, passed)]].set(jnp.asarray(sizes, jnp.int32))

    sizes = jnp.where(number % 4 == 0, named(heavy_load, number // 4), named(common, number - number // 4 - 1))
    mixed = jax.random.permutation(jax.random.fold_in(own, 3), count)
    donor, sink = mixed[0:count // 2 * 2:2], mixed[1:count // 2 * 2:2]
    slack = jnp.minimum(sizes[donor] - 1, most - sizes[sink]) // 2
    slack = jnp.where((donor == sequence[0]) | (sink == sequence[0]) | (sizes[sink] == 0), 0, jnp.maximum(slack, 0))
    passed = jax.random.randint(jax.random.fold_in(own, 4), (count // 2,), 0, 1 << 20) % (slack + 1)
    sizes = sizes.at[donor].add(-passed).at[sink].add(passed)
    labels = jnp.searchsorted(jnp.cumsum(sizes), jnp.arange(rows * top), side="right").astype(jnp.int32)
    listing = labels.reshape(top, rows).T
    listing = listing[jax.random.permutation(jax.random.fold_in(own, 1), rows)]
    turn = jax.random.randint(jax.random.fold_in(own, 2), (rows, 1), 0, top)
    return jnp.take_along_axis(listing, (jnp.arange(top)[None, :] + turn) % top, axis=1)


def shares(number_of, total, reach, skew, full):
    loads = [(1 << 20) // math.isqrt(standing ** skew) + 1 for standing in range(1, number_of + 1)]
    largest = reach if full else min(reach, max(-(-total // number_of), total * loads[0] // sum(loads)))
    least = 1 if total - largest >= number_of - 1 else 0
    given, rest = [largest] + [least] * (number_of - 1), total - largest - least * (number_of - 1)
    while rest > 0:
        free = [i for i in range(1, number_of) if given[i] < largest] or [i for i in range(1, number_of) if given[i] < reach]
        pool, left = sum([loads[i] for i in free]), rest
        for i in free:
            extra = min(reach - given[i], max(1, left * loads[i] // pool), rest)
            given[i] = given[i] + extra
            rest = rest - extra
    return np.array(given)


def setup_inputs(seed: int = 0) -> dict:
    streams_of = jax.random.split(jax.random.key(seed), 6)
    hidden = draw_hidden(jax.random.fold_in(streams_of[5], 71), 0)
    flags_keys = jax.random.split(jax.random.fold_in(streams_of[1], 1), ROWS // ROW_GRP)
    flags_turns = jax.random.permutation(jax.random.fold_in(streams_of[1], 3), ROWS // ROW_GRP)
    flags = jax.vmap(lambda own, number: shared_out(jax.random.fold_in(streams_of[1], 2), own, number, ROW_GRP, SHARDS + 1, 1, CAP, 2))(flags_keys, flags_turns).reshape((ROWS, 1))
    targets = plant(ranked_ids(streams_of[2], (ROWS,), VOCAB, 2), jax.random.fold_in(streams_of[2], 3), 0, VOCAB - 1).astype(jnp.int32)
    head = draw_head(jax.random.fold_in(streams_of[5], 71), 0)
    lengths = jax.vmap(lambda own: uneven_parts(own, DOCS, ROW_GRP, ROW_GRP // 2, 2))(jax.random.split(streams_of[4], SHARDS)).reshape((SHARDS, DOCS)).astype(jnp.int32)
    return dict(hidden=hidden, flags=flags, targets=targets, head=head, lengths=lengths)


def slot_table(flag_col, groups, capacity, shard_rows):
    values = jnp.arange(groups + 1, dtype=jnp.int32)
    onehot = (flag_col[:, None] == values[None, :]).astype(jnp.int32)
    ranking = lax.optimization_barrier(jnp.sum((jnp.cumsum(onehot, axis=0) - 1) * onehot, axis=1))
    where_to = jnp.where(flag_col < groups, flag_col * capacity + ranking, groups * capacity)
    table = jnp.full((groups * capacity + 1,), -1, jnp.int32)
    table = table.at[where_to].set(jnp.arange(shard_rows, dtype=jnp.int32))
    return table[:groups * capacity]

def reference(hidden, flags, targets, head, lengths):
    groups = SHARDS
    capacity = CAP
    shard_rows = ROW_GRP
    tables = jnp.stack([slot_table(flags[s * shard_rows:(s + 1) * shard_rows, 0], groups, capacity, shard_rows) for s in range(groups)])
    src_grid = tables.reshape(groups, groups, capacity).transpose(1, 0, 2)
    offsets = (jnp.arange(groups, dtype=jnp.int32) * shard_rows)[None, :, None]
    is_live = (src_grid >= 0).reshape(-1)
    row_index = jnp.where(src_grid >= 0, src_grid + offsets, 0).reshape(-1).astype(jnp.int32)
    scored = jnp.where(is_live[:, None], hidden[row_index], jnp.zeros((), jnp.bfloat16))
    target_ids = jnp.where(is_live, targets[row_index], -1)
    vocab_step = min(VOCAB, 4096)

    def one_block(index):
        weights = lax.dynamic_slice_in_dim(head, index * vocab_step, vocab_step, 1)
        return jnp.dot(scored, weights, preferred_element_type=jnp.float32)
    blocks = lax.map(one_block, jnp.arange(VOCAB // vocab_step, dtype=jnp.int32))
    logits = blocks.transpose(1, 0, 2).reshape(scored.shape[0], VOCAB)
    row_max = lax.optimization_barrier(jnp.max(logits, axis=1))
    shifted = logits - row_max[:, None]
    scaled = jnp.exp(shifted)
    row_total = lax.optimization_barrier(jnp.sum(scaled, axis=1))
    first_mom = lax.optimization_barrier(jnp.sum(scaled * shifted, axis=1))
    second_mom = lax.optimization_barrier(jnp.sum(scaled * shifted * shifted, axis=1))
    mean_shift = first_mom / row_total
    row_var = second_mom / row_total - mean_shift * mean_shift
    target_val = jnp.take_along_axis(logits, jnp.maximum(target_ids, 0)[:, None], axis=1)[:, 0]
    token_scores = jnp.where(target_ids >= 0, (target_val - row_max - mean_shift) / jnp.sqrt(jnp.maximum(row_var, 1.0)), jnp.float32(0.0))
    by_grid = token_scores.reshape(groups, groups, capacity)
    doc_list = []
    for s in range(groups):
        returned = by_grid[:, s, :].reshape(-1)
        table = tables[s]
        row_val = jnp.zeros((shard_rows + 1,), jnp.float32).at[jnp.where(table >= 0, table, shard_rows)].set(returned)[:shard_rows]
        flagged = (flags[s * shard_rows:(s + 1) * shard_rows, 0] < groups).astype(jnp.float32)
        doc_ends = jnp.cumsum(lengths[s])
        doc_starts = doc_ends - lengths[s]
        positions = jnp.arange(shard_rows, dtype=jnp.int32)
        membership = ((positions[None, :] >= doc_starts[:, None]) & (positions[None, :] < doc_ends[:, None])).astype(jnp.float32)
        sums = lax.optimization_barrier(jnp.sum(membership * row_val[None, :], axis=1))
        counts = lax.optimization_barrier(jnp.sum(membership * flagged[None, :], axis=1))
        doc_list.append(sums / jnp.maximum(counts, 1.0))
    return (token_scores, jnp.stack(doc_list))
```

```python
import jax
import jax.numpy as jnp
from jax import lax
from jax.experimental import pallas as pl
from jax.experimental.pallas import tpu as pltpu
from jax.sharding import PartitionSpec as P

MESH = pl.DeviceIdType.MESH
F32, BF16, I32, I16 = jnp.float32, jnp.bfloat16, jnp.int32, jnp.int16

NX, NC, NY, NZ = 4, 2, 4, 8
R = 128
FEAT = 512
HALF = FEAT // 2
KB = 2048
VB = 2048
TN = 512
NT = VB // TN
CAP = 16
OFF = (2, 1, 3, 0)
CODE_MAX = 32767.0
UNIT = 0.4375
EXT = 128

EARLY = tuple((k, s - k) for s in range(5) for k in range(4) if 0 <= s - k <= 4)
LATE = tuple((k, s - k) for s in range(5, 8) for k in range(4) if 0 <= s - k <= 4)


def rem(a, n):
    return lax.rem(a, jnp.int32(n))


def div(a, n):
    return lax.div(a, jnp.int32(n))


def body(
    hidden, head, flags, targets, lengths, tok_out, doc_out,
    X, W, Pb, PR, Q0, Q1, Q2, C0, C1, C2, stats, ST, SR, FS, FB, SS, SC, slots,
    w_sem, s1_send, s1_recv, z_send, z_recv, y_send, y_recv, p_send, p_recv,
    q_send, q_recv, st_send, st_recv, sc_send, sc_recv, f_send, f_recv,
):
    g = lax.axis_index("grp")
    v = lax.axis_index("vocab")
    x, c = div(g, NC), rem(g, NC)
    y, z = div(v, NZ), rem(v, NZ)
    rel = rem(z - 4 * c + NZ, NZ)
    h = rem(y, 2)
    plane = div(z, 4)

    def remote(src, dst, ss, rs, gg, vv):
        return pltpu.make_async_remote_copy(
            src_ref=src, dst_ref=dst, send_sem=ss, recv_sem=rs,
            device_id=(gg, vv), device_id_type=MESH,
        )

    def w_copy(j):
        return pltpu.make_async_copy(
            head.at[pl.ds(j * 512, 512)], W.at[pl.ds(j * 512, 512)], w_sem.at[j]
        )

    for j in range(4):
        w_copy(j).start()
    FS[...] = jnp.broadcast_to(flags[...], (8, R))

    barrier = pltpu.get_barrier_semaphore()

    def hello(gg, vv):
        pl.semaphore_signal(barrier, inc=1, device_id=(gg, vv), device_id_type=MESH)

    def hello_plane(i, _):
        hello(g, rem(v + i, NY * NZ))
        return 0

    def hello_grp(i, _):
        hello(rem(g + i, NX * NC), v)
        return 0

    lax.fori_loop(1, NX * NC, hello_grp, 0)

    @pl.when(plane == c)
    def _():
        def hello_source(r, _):
            @pl.when(jnp.logical_not((r == g) & (x == y)))
            def _():
                hello(r, x * NZ + z)
            return 0

        lax.fori_loop(0, NX * NC, hello_source, 0)

    lax.fori_loop(1, NY * NZ, hello_plane, 0)
    mine = ((x == y) & (plane == c)).astype(I32)
    pl.semaphore_wait(barrier, NY * NZ - 1 + NX * NC - 1 + NY - mine)

    g1 = y * 2 + plane
    j1 = rem(z, 4)

    def s1_refs(yy):
        hh = yy % 2
        return (
            hidden.at[:, pl.ds(hh * HALF, HALF)],
            X.at[g, :, pl.ds(pl.multiple_of(j1 * FEAT + hh * HALF, HALF), HALF)],
        )

    def s1_copy(yy):
        src, dst = s1_refs(yy)
        return remote(src, dst, s1_send.at[yy], s1_recv.at[g], g1, yy * NZ + z)

    def s1_self(yy):
        return (g1 == g) & (y == yy)

    for yy in range(NY):
        @pl.when(jnp.logical_not(s1_self(yy)))
        def _(yy=yy):
            s1_copy(yy).start()

        @pl.when(s1_self(yy))
        def _(yy=yy):
            src, dst = s1_refs(yy)
            pltpu.make_async_copy(src, dst, s1_recv.at[g]).start()

    def f_copy(i):
        return remote(FS, FB.at[g], f_send.at[i], f_recv.at[g], rem(g + i, NX * NC), v)

    def f_start(i, _):
        f_copy(i).start()
        return 0

    lax.fori_loop(1, NX * NC, f_start, 0)
    FB[g] = FS[...]

    def chunk_at(k):
        return rem(x + OFF[k], NX)

    def unit(k, cp, j, hh):
        col = pl.multiple_of(j * FEAT + hh * HALF, HALF)
        return X.at[2 * chunk_at(k) + cp, :, pl.ds(col, HALF)]

    def z_copy(k, t, way, cp, j):
        ref = unit(k, cp, j, h)
        to = rem(z + (1 if way == 0 else NZ - 1), NZ)
        return remote(ref, ref, z_send.at[k, t, way, cp], z_recv.at[k, cp, j], g, y * NZ + to)

    def y_copy(k, cp, j):
        ref = unit(k, cp, j, h)
        to = rem(y + (1 if cp == 0 else NY - 1), NY)
        return remote(ref, ref, y_send.at[k, cp, j], y_recv.at[k, cp, j], g, to * NZ + z)

    reach = ((4, 3), (3, 4))

    def origin(t, way):
        return rem(rel + (NZ - t if way == 0 else t), NZ)

    def event(k, t):
        if t == 0:
            @pl.when(rel < 4)
            def _():
                for cp in range(2):
                    r = 2 * chunk_at(k) + cp
                    ref = unit(k, cp, rel, h)
                    pltpu.make_async_copy(ref, ref, s1_recv.at[r]).wait()
                    z_copy(k, 0, 0, cp, rel).start()
                    z_copy(k, 0, 1, cp, rel).start()
                    y_copy(k, cp, rel).start()
            return
        for way in range(2):
            j = origin(t, way)

            @pl.when(j < 4)
            def _(way=way, j=j):
                for cp in range(2):
                    if t > reach[way][cp]:
                        continue
                    ref = unit(k, cp, j, h)
                    remote(ref, ref, z_send.at[k, 0, way, cp], z_recv.at[k, cp, j], g, v).wait_recv()
                    if t < reach[way][cp]:
                        z_copy(k, t, way, cp, j).start()
                    y_copy(k, cp, j).start()

    for k, t in EARLY:
        event(k, t)
    for j in range(4):
        w_copy(j).wait()

    def p_copy(k, n):
        cols = pl.ds(pl.multiple_of(n * TN, TN), TN)
        return remote(
            Pb.at[k, 1 - c, :, cols], PR.at[k, :, cols],
            p_send.at[k, n], p_recv.at[k, n], x * NC + (1 - c), v,
        )

    def wait_y(k):
        for cp in range(2):
            for j in range(4):
                ref = unit(k, cp, j, 1 - h)
                remote(ref, ref, y_send.at[k, cp, j], y_recv.at[k, cp, j], g, v).wait_recv()

    right, left = rem(x + 1, NX) * NC + c, rem(x + NX - 1, NX) * NC + c
    HV = VB // 2

    def q_copies(k):
        if k == 0:
            return (
                remote(Q0.at[0], C0.at[0], q_send.at[0], q_recv.at[0], right, v),
                remote(Q0.at[1], C0.at[1], q_send.at[1], q_recv.at[1], left, v),
            )
        if k == 1:
            return (remote(Q1, C1, q_send.at[2], q_recv.at[2], right, v),)
        return (remote(Q2, C2, q_send.at[3], q_recv.at[3], left, v),)

    def decode(block):
        wide = block.astype(I32).astype(F32)
        cols = wide.shape[1] - EXT
        step = wide[:, cols:cols + 1] * (UNIT / CODE_MAX)
        return wide[:, :cols] * step

    def encode(total):
        top = jnp.max(jnp.abs(total), axis=1, keepdims=True)
        scale = jnp.maximum(jnp.ceil(top * (1.0 / UNIT)), 1.0)
        codes = jnp.round(total * (CODE_MAX / (scale * UNIT)))
        return (
            codes.astype(I32).astype(I16),
            jnp.broadcast_to(scale, (total.shape[0], EXT)).astype(I32).astype(I16),
        )

    def pair_sum(k, rows):
        return Pb[k, c, rows, :] + PR[k, rows, :]

    def wait_pair(k):
        for n in range(NT):
            p_copy(k, n).wait_recv()

    def post(k):
        wait_pair(k)
        if k == 1:
            q_copies(0)[0].wait_recv()
        if k == 2:
            q_copies(0)[1].wait_recv()

        @pl.loop(0, R // 16)
        def _(i):
            rows = pl.ds(pl.multiple_of(i * 16, 16), 16)
            total = pair_sum(k, rows)
            if k == 0:
                codes, scale = encode(total)
                for side in range(2):
                    Q0[side, rows, :HV] = codes[:, side * HV:(side + 1) * HV]
                    Q0[side, rows, HV:] = scale
            else:
                first, second = total[:, :HV], total[:, HV:]
                if k == 1:
                    first = first + decode(C0[0, rows, :])
                else:
                    second = second + decode(C0[1, rows, :])
                codes, scale = encode(jnp.concatenate([first, second], axis=1))
                out = Q1 if k == 1 else Q2
                out[rows, :VB] = codes
                out[rows, VB:] = scale

        for copy in q_copies(k):
            copy.start()

    late = {}
    for at, ev in enumerate(LATE):
        late.setdefault(at, []).append(ev)

    def tile(step, _):
        k, n = div(step, NT), rem(step, NT)
        for kk in range(4):
            @pl.when(step == kk * NT)
            def _(kk=kk):
                wait_y(kk)
        d = rem(x + jnp.where(k == 0, 2, jnp.where(k == 1, 1, jnp.where(k == 2, 3, 0))), NX)
        cols = pl.ds(pl.multiple_of(n * TN, TN), TN)
        rows = X[pl.ds(2 * d, 2)].reshape(2 * R, KB)
        out = jnp.dot(rows, W[:, cols], preferred_element_type=F32)
        Pb[k, :, :, cols] = out.reshape(2, R, TN)
        p_copy(k, n).start()
        for at, events in late.items():
            @pl.when(step == at)
            def _(events=events):
                for ev in events:
                    event(*ev)
        for kk in range(3):
            @pl.when(step == (kk + 1) * NT + 1)
            def _(kk=kk):
                post(kk)
        return 0

    lax.fori_loop(0, 4 * NT, tile, 0)

    def f_wait(i, _):
        gg = rem(g + i, NX * NC)
        remote(FS, FB.at[gg], f_send.at[0], f_recv.at[gg], gg, v).wait_recv()
        return 0

    lax.fori_loop(1, NX * NC, f_wait, 0)
    named = FB[:, 0, :] == g
    above = (
        lax.broadcasted_iota(I32, (R, R), 0) < lax.broadcasted_iota(I32, (R, R), 1)
    ).astype(BF16)
    rank = jnp.dot(named.astype(F32).astype(BF16), above, preferred_element_type=F32)
    shard = lax.broadcasted_iota(I32, (8, R), 0)
    slots[...] = jnp.where(named, shard * CAP + rank.astype(I32), -1)

    wait_pair(3)
    q_copies(1)[0].wait_recv()
    q_copies(2)[0].wait_recv()
    want = jnp.transpose(jnp.broadcast_to(targets[...].astype(F32), (R, R)))
    stats[...] = want

    @pl.loop(0, R // 16)
    def _(i):
        rows = pl.ds(pl.multiple_of(i * 16, 16), 16)
        logits = pair_sum(3, rows) + decode(C1[rows, :]) + decode(C2[rows, :])
        target = stats[rows, :][:, :1].astype(I32) - v * VB
        top = jnp.max(logits, axis=1, keepdims=True)
        shifted = logits - top
        scaled = jnp.exp(shifted)
        first = scaled * shifted
        total = jnp.sum(scaled, axis=1, keepdims=True)
        mom1 = jnp.sum(first, axis=1, keepdims=True)
        mom2 = jnp.sum(first * shifted, axis=1, keepdims=True)
        column = lax.broadcasted_iota(I32, (16, VB), 1)
        val = jnp.sum(jnp.where(column == target, logits, 0.0), axis=1, keepdims=True)
        lane = lax.broadcasted_iota(I32, (16, R), 1)
        stats[rows, :] = jnp.where(
            lane == 0, top,
            jnp.where(lane == 1, total, jnp.where(lane == 2, mom1, jnp.where(lane == 3, mom2, val))),
        )

    ST[...] = jnp.transpose(stats[...])[:8, :]
    SR[v] = ST[...]

    def st_copy(i):
        return remote(ST, SR.at[v], st_send.at[i], st_recv.at[v], g, rem(v + i, NY * NZ))

    def st_start(i, _):
        st_copy(i).start()
        return 0

    lax.fori_loop(1, NY * NZ, st_start, 0)

    def st_wait(i, _):
        vv = rem(v + i, NY * NZ)
        remote(ST, SR.at[vv], st_send.at[0], st_recv.at[vv], g, v).wait_recv()
        return 0

    lax.fori_loop(1, NY * NZ, st_wait, 0)
    tops = SR[:, 0, :]
    top = jnp.max(tops, axis=0, keepdims=True)
    gap = tops - top
    fac = jnp.exp(gap)
    tot, m1, m2 = SR[:, 1, :], SR[:, 2, :], SR[:, 3, :]
    total = jnp.sum(fac * tot, axis=0, keepdims=True)
    mom1 = jnp.sum(fac * (m1 + gap * tot), axis=0, keepdims=True)
    mom2 = jnp.sum(fac * (m2 + 2.0 * gap * m1 + gap * gap * tot), axis=0, keepdims=True)
    val = jnp.sum(SR[:, 4, :], axis=0, keepdims=True)
    mean = mom1 / total
    var = mom2 / total - mean * mean
    score = (val - top - mean) / jnp.sqrt(jnp.maximum(var, 1.0))

    SS[...] = jnp.broadcast_to(score, (8, R))
    SC[g] = SS[...]

    def sc_copy(i):
        return remote(SS, SC.at[g], sc_send.at[i], sc_recv.at[g], rem(g + i, NX * NC), v)

    def sc_start(i, _):
        sc_copy(i).start()
        return 0

    lax.fori_loop(1, NX * NC, sc_start, 0)

    ends_of = jnp.broadcast_to(lengths[...], (8, 8))
    doc = lax.broadcasted_iota(I32, (8, 8), 0)
    at = lax.broadcasted_iota(I32, (8, 8), 1)
    ends = jnp.sum(jnp.where(at <= doc, ends_of, 0), axis=1, keepdims=True)
    starts = jnp.sum(jnp.where(at < doc, ends_of, 0), axis=1, keepdims=True)
    position = lax.broadcasted_iota(I32, (8, R), 1)
    member = (position >= starts) & (position < ends) & (flags[...] < NX * NC)
    sums = jnp.sum(jnp.where(member, SS[...], 0.0), axis=1, keepdims=True)
    counts = jnp.sum(jnp.where(member, 1.0, 0.0), axis=1, keepdims=True)
    means = sums / jnp.maximum(counts, 1.0)
    doc_out[...] = jnp.sum(jnp.where(at == doc, means, 0.0), axis=0, keepdims=True)

    def sc_wait(i, _):
        gg = rem(g + i, NX * NC)
        remote(SS, SC.at[gg], sc_send.at[0], sc_recv.at[gg], gg, v).wait_recv()
        return 0

    lax.fori_loop(1, NX * NC, sc_wait, 0)
    place = lax.broadcasted_iota(I32, (R, R), 0)
    spread = jnp.zeros((R, R), F32)
    for s in range(8):
        spread = spread + jnp.where(slots[s:s + 1, :] == place, SC[s, 0:1, :], 0.0)
    tok_out[...] = jnp.sum(jnp.transpose(spread), axis=0, keepdims=True)

    for yy in range(NY):
        @pl.when(jnp.logical_not(s1_self(yy)))
        def _(yy=yy):
            s1_copy(yy).wait_send()

    for k in range(4):
        @pl.when(rel < 4)
        def _(k=k):
            for cp in range(2):
                z_copy(k, 0, 0, cp, rel).wait_send()
                z_copy(k, 0, 1, cp, rel).wait_send()
        for t in range(1, 4):
            for way in range(2):
                j = origin(t, way)

                @pl.when(j < 4)
                def _(k=k, t=t, way=way, j=j):
                    for cp in range(2):
                        if t < reach[way][cp]:
                            z_copy(k, t, way, cp, j).wait_send()
        for cp in range(2):
            for j in range(4):
                y_copy(k, cp, j).wait_send()
        for n in range(NT):
            p_copy(k, n).wait_send()
        if k < 3:
            for copy in q_copies(k):
                copy.wait_send()

    def st_sent(i, _):
        st_copy(i).wait_send()
        return 0

    def sc_sent(i, _):
        f_copy(i).wait_send()
        sc_copy(i).wait_send()
        return 0

    lax.fori_loop(1, NY * NZ, st_sent, 0)
    lax.fori_loop(1, NX * NC, sc_sent, 0)


def shards(hidden, flags, targets, head, lengths):
    vmem = pl.BlockSpec(memory_space=pltpu.VMEM)
    anywhere = pl.BlockSpec(memory_space=pl.ANY)
    dma = pltpu.SemaphoreType.DMA
    tok, doc = pl.pallas_call(
        body,
        out_shape=(
            jax.ShapeDtypeStruct((1, R), F32),
            jax.ShapeDtypeStruct((1, 8), F32),
        ),
        in_specs=[anywhere, anywhere, vmem, vmem, vmem],
        out_specs=(vmem, vmem),
        scratch_shapes=[
            pltpu.VMEM((8, R, KB), BF16),
            pltpu.VMEM((KB, VB), BF16),
            pltpu.VMEM((4, 2, R, VB), F32),
            pltpu.VMEM((4, R, VB), F32),
            pltpu.VMEM((2, R, VB // 2 + EXT), I16),
            pltpu.VMEM((R, VB + EXT), I16),
            pltpu.VMEM((R, VB + EXT), I16),
            pltpu.VMEM((2, R, VB // 2 + EXT), I16),
            pltpu.VMEM((R, VB + EXT), I16),
            pltpu.VMEM((R, VB + EXT), I16),
            pltpu.VMEM((R, R), F32),
            pltpu.VMEM((8, R), F32),
            pltpu.VMEM((NY * NZ, 8, R), F32),
            pltpu.VMEM((8, R), I32),
            pltpu.VMEM((8, 8, R), I32),
            pltpu.VMEM((8, R), F32),
            pltpu.VMEM((8, 8, R), F32),
            pltpu.VMEM((8, R), I32),
            dma((4,)), dma((4,)), dma((8,)),
            dma((4, 4, 2, 2)), dma((4, 2, 4)),
            dma((4, 2, 4)), dma((4, 2, 4)),
            dma((4, NT)), dma((4, NT)),
            dma((4,)), dma((4,)),
            dma((32,)), dma((32,)),
            dma((8,)), dma((8,)), dma((8,)), dma((8,)),
        ],
        compiler_params=pltpu.CompilerParams(
            collective_id=0, has_side_effects=True, vmem_limit_bytes=60 * 1024 * 1024
        ),
        name="score",
    )(hidden, head, flags.reshape(1, R), targets.reshape(1, R), lengths)
    return tok.reshape(R), doc


def solution(mesh):
    placed = (P("grp", "vocab"), P("grp", None), P("grp"), P("grp", "vocab"), P("grp", None))
    return jax.shard_map(
        shards, mesh=mesh, in_specs=placed, out_specs=(P("grp"), P("grp", None)), check_vma=False
    )
```

```python
import jax
import jax.numpy as jnp
from jax import lax
from jax.experimental import pallas as pl
from jax.experimental.pallas import tpu as pltpu
from jax.sharding import PartitionSpec as P

MESH = pl.DeviceIdType.MESH
F32, BF16, I32, I16 = jnp.float32, jnp.bfloat16, jnp.int32, jnp.int16

NX, NC, NY, NZ = 4, 2, 4, 8
R = 128
FEAT = 512
HALF = FEAT // 2
KB = 2048
VB = 2048
TN = 512
NT = VB // TN
CAP = 16
OFF = (2, 1, 3, 0)
CODE_MAX = 32767.0
UNIT = 0.4375
EXT = 128

HV = VB // 2

ORDER = sorted(((k, t) for k in range(4) for t in range(5)), key=lambda e: (2 * e[1] + e[0], e[0]))
EARLY = tuple(ORDER[:16])
LATE = {0: (ORDER[16],), 1: (ORDER[17],), 3: (ORDER[18],), 6: (ORDER[19],)}
POSTS = {3: ((0, 0),), 5: ((0, 1),), 7: ((1, 1),), 11: ((2, 0), (1, 0)), 13: ((2, 1),)}


def rem(a, n):
    return lax.rem(a, jnp.int32(n))


def div(a, n):
    return lax.div(a, jnp.int32(n))


def body(
    hidden, head, flags, targets, lengths, result,
    X, W, H, Pb, PR, Q, C, stats, ST, SR, FS, FB, SS, SC, slots,
    w_sem, h_send, h_recv, s1_send, s1_recv, z_send, z_recv, y_send, y_recv, p_send, p_recv,
    q_send, q_recv, st_send, st_recv, sc_send, sc_recv, f_send, f_recv,
):
    g = lax.axis_index("grp")
    v = lax.axis_index("vocab")
    x, c = div(g, NC), rem(g, NC)
    y, z = div(v, NZ), rem(v, NZ)
    rel = rem(z - 4 * c + NZ, NZ)
    h = rem(y, 2)
    plane = div(z, 4)

    def remote(src, dst, ss, rs, gg, vv):
        return pltpu.make_async_remote_copy(
            src_ref=src, dst_ref=dst, send_sem=ss, recv_sem=rs,
            device_id=(gg, vv), device_id_type=MESH,
        )

    def w_copy(j):
        return pltpu.make_async_copy(
            head.at[pl.ds(j * 512, 512)], W.at[pl.ds(j * 512, 512)], w_sem.at[j]
        )

    def half_of(side):
        return hidden.at[:, pl.ds(pl.multiple_of(side * HALF, HALF), HALF)]

    pltpu.make_async_copy(half_of(h), H.at[y], h_recv.at[y]).start()
    for j in range(4):
        w_copy(j).start()
    FS[...] = jnp.broadcast_to(flags[...], (8, R))

    barrier = pltpu.get_barrier_semaphore()

    def hello(gg, vv):
        pl.semaphore_signal(barrier, inc=1, device_id=(gg, vv), device_id_type=MESH)

    def hello_plane(i, _):
        hello(g, rem(v + i, NY * NZ))
        return 0

    def hello_grp(i, _):
        hello(rem(g + i, NX * NC), v)
        return 0

    lax.fori_loop(1, NX * NC, hello_grp, 0)

    lax.fori_loop(1, NY * NZ, hello_plane, 0)
    pl.semaphore_wait(barrier, NY * NZ - 1 + NX * NC - 1)

    j1 = rem(z, 4)

    def h_copy(i):
        yy = rem(y + i, NY)
        return remote(half_of(rem(yy, 2)), H.at[y], h_send.at[i], h_recv.at[y], g, yy * NZ + z)

    for i in (2, 1, 3):
        h_copy(i).start()

    def s1_owner(i):
        return rem(x + i, NX) * NC + plane

    def s1_refs(i):
        col = pl.multiple_of(j1 * FEAT + h * HALF, HALF)
        return H.at[rem(x + i, NX)], X.at[g, :, pl.ds(col, HALF)]

    def s1_copy(i):
        src, dst = s1_refs(i)
        return remote(src, dst, s1_send.at[i], s1_recv.at[g], s1_owner(i), v)

    for i in (2, 3, 1, 0):
        src, dst = s1_refs(i)
        pltpu.make_async_copy(src, src, h_recv.at[rem(x + i, NX)]).wait()
        if i:
            s1_copy(i).start()
            continue

        @pl.when(plane == c)
        def _(src=src, dst=dst):
            pltpu.make_async_copy(src, dst, s1_recv.at[g]).start()

        @pl.when(plane != c)
        def _():
            s1_copy(0).start()

    def f_copy(i):
        return remote(FS, FB.at[g], f_send.at[i], f_recv.at[g], rem(g + i, NX * NC), v)

    def f_start(i, _):
        f_copy(i).start()
        return 0

    lax.fori_loop(1, NX * NC, f_start, 0)
    FB[g] = FS[...]

    def chunk_at(k):
        return rem(x + OFF[k], NX)

    def unit(k, cp, j, hh):
        col = pl.multiple_of(j * FEAT + hh * HALF, HALF)
        return X.at[2 * chunk_at(k) + cp, :, pl.ds(col, HALF)]

    def z_copy(k, t, way, cp, j):
        ref = unit(k, cp, j, h)
        to = rem(z + (1 if way == 0 else NZ - 1), NZ)
        return remote(ref, ref, z_send.at[k, t, way, cp], z_recv.at[k, cp, j], g, y * NZ + to)

    def y_copy(k, cp, j):
        ref = unit(k, cp, j, h)
        to = rem(y + (1 if cp == 0 else NY - 1), NY)
        return remote(ref, ref, y_send.at[k, cp, j], y_recv.at[k, cp, j], g, to * NZ + z)

    reach = ((4, 3), (3, 4))

    def origin(t, way):
        return rem(rel + (NZ - t if way == 0 else t), NZ)

    def event(k, t):
        if t == 0:
            @pl.when(rel < 4)
            def _():
                for cp in range(2):
                    r = 2 * chunk_at(k) + cp
                    ref = unit(k, cp, rel, h)
                    pltpu.make_async_copy(ref, ref, s1_recv.at[r]).wait()
                    z_copy(k, 0, 0, cp, rel).start()
                    z_copy(k, 0, 1, cp, rel).start()
                    y_copy(k, cp, rel).start()
            return
        for way in range(2):
            j = origin(t, way)

            @pl.when(j < 4)
            def _(way=way, j=j):
                for cp in range(2):
                    if t > reach[way][cp]:
                        continue
                    ref = unit(k, cp, j, h)
                    remote(ref, ref, z_send.at[k, 0, way, cp], z_recv.at[k, cp, j], g, v).wait_recv()
                    if t < reach[way][cp]:
                        z_copy(k, t, way, cp, j).start()
                    y_copy(k, cp, j).start()

    for k, t in EARLY:
        event(k, t)
    for j in range(4):
        w_copy(j).wait()

    def p_copy(k, n):
        cols = pl.ds(pl.multiple_of(n * TN, TN), TN)
        return remote(
            Pb.at[k, 1 - c, :, cols], PR.at[k, :, cols],
            p_send.at[k, n], p_recv.at[k, n], x * NC + (1 - c), v,
        )

    def wait_y(k):
        for cp in range(2):
            for j in range(4):
                ref = unit(k, cp, j, 1 - h)
                remote(ref, ref, y_send.at[k, cp, j], y_recv.at[k, cp, j], g, v).wait_recv()

    right, left = rem(x + 1, NX) * NC + c, rem(x + NX - 1, NX) * NC + c

    def q_copy(k, hf):
        u = 2 * k + hf
        to = right if k == 1 or (k == 0 and hf == 0) else left
        return remote(Q.at[u], C.at[u], q_send.at[u], q_recv.at[u], to, v)

    def decode(u, rows):
        wide = C[u, rows, :].astype(I32).astype(F32)
        return wide[:, :HV] * (wide[:, HV:HV + 1] * (UNIT / CODE_MAX))

    def encode(total):
        top = jnp.max(jnp.abs(total), axis=1, keepdims=True)
        scale = jnp.maximum(jnp.ceil(top * (1.0 / UNIT)), 1.0)
        codes = jnp.round(total * (CODE_MAX / (scale * UNIT)))
        return (
            codes.astype(I32).astype(I16),
            jnp.broadcast_to(scale, (total.shape[0], EXT)).astype(I32).astype(I16),
        )

    def pair_sum(k, rows, hf):
        cols = slice(hf * HV, (hf + 1) * HV)
        return Pb[k, c, rows, cols] + PR[k, rows, cols]

    def wait_pair(k, hf):
        for n in (2 * hf, 2 * hf + 1):
            p_copy(k, n).wait_recv()

    def post(k, hf):
        wait_pair(k, hf)
        relayed = k == hf + 1
        if relayed:
            q_copy(0, hf).wait_recv()
        u = 2 * k + hf

        @pl.loop(0, R // 16)
        def _(i):
            rows = pl.ds(pl.multiple_of(i * 16, 16), 16)
            total = pair_sum(k, rows, hf)
            if relayed:
                total = total + decode(hf, rows)
            codes, scale = encode(total)
            Q[u, rows, :HV] = codes
            Q[u, rows, HV:] = scale

        q_copy(k, hf).start()

    def tile(step, _):
        k = div(step, NT)
        n = rem(step + jnp.where(k == 1, 2, 0), NT)
        for kk in range(4):
            @pl.when(step == kk * NT)
            def _(kk=kk):
                wait_y(kk)
        d = rem(x + jnp.where(k == 0, 2, jnp.where(k == 1, 1, jnp.where(k == 2, 3, 0))), NX)
        cols = pl.ds(pl.multiple_of(n * TN, TN), TN)
        rows = X[pl.ds(2 * d, 2)].reshape(2 * R, KB)
        out = jnp.dot(rows, W[:, cols], preferred_element_type=F32)
        Pb[k, :, :, cols] = out.reshape(2, R, TN)
        p_copy(k, n).start()
        for at, events in LATE.items():
            @pl.when(step == at)
            def _(events=events):
                for ev in events:
                    event(*ev)
        for at, blocks in POSTS.items():
            @pl.when(step == at)
            def _(blocks=blocks):
                for block in blocks:
                    post(*block)
        return 0

    lax.fori_loop(0, 4 * NT, tile, 0)

    def f_wait(i, _):
        gg = rem(g + i, NX * NC)
        remote(FS, FB.at[gg], f_send.at[0], f_recv.at[gg], gg, v).wait_recv()
        return 0

    lax.fori_loop(1, NX * NC, f_wait, 0)
    named = FB[:, 0, :] == g
    above = (
        lax.broadcasted_iota(I32, (R, R), 0) < lax.broadcasted_iota(I32, (R, R), 1)
    ).astype(BF16)
    rank = jnp.dot(named.astype(F32).astype(BF16), above, preferred_element_type=F32)
    shard = lax.broadcasted_iota(I32, (8, R), 0)
    slots[...] = jnp.where(named, shard * CAP + rank.astype(I32), -1)

    for hf in range(2):
        wait_pair(3, hf)
    want = jnp.transpose(jnp.broadcast_to(targets[...].astype(F32), (R, R)))
    stats[...] = want
    for hf in (1, 0):
        q_copy(1, hf).wait_recv()

        @pl.loop(0, R // 16)
        def _(i, hf=hf):
            rows = pl.ds(pl.multiple_of(i * 16, 16), 16)
            PR[3, rows, hf * HV:(hf + 1) * HV] = pair_sum(3, rows, hf) + decode(2 + hf, rows)

    for hf in range(2):
        q_copy(2, hf).wait_recv()

    @pl.loop(0, R // 16)
    def _(i):
        rows = pl.ds(pl.multiple_of(i * 16, 16), 16)
        logits = PR[3, rows, :] + jnp.concatenate([decode(4, rows), decode(5, rows)], axis=1)
        target = stats[rows, :][:, :1].astype(I32) - v * VB
        top = jnp.max(logits, axis=1, keepdims=True)
        shifted = logits - top
        scaled = jnp.exp(shifted)
        first = scaled * shifted
        total = jnp.sum(scaled, axis=1, keepdims=True)
        mom1 = jnp.sum(first, axis=1, keepdims=True)
        mom2 = jnp.sum(first * shifted, axis=1, keepdims=True)
        column = lax.broadcasted_iota(I32, (16, VB), 1)
        val = jnp.sum(jnp.where(column == target, logits, 0.0), axis=1, keepdims=True)
        lane = lax.broadcasted_iota(I32, (16, R), 1)
        stats[rows, :] = jnp.where(
            lane == 0, top,
            jnp.where(lane == 1, total, jnp.where(lane == 2, mom1, jnp.where(lane == 3, mom2, val))),
        )

    ST[...] = jnp.transpose(stats[...])[:8, :]
    SR[v] = ST[...]

    def st_copy(i):
        return remote(ST, SR.at[v], st_send.at[i], st_recv.at[v], g, rem(v + i, NY * NZ))

    def st_start(i, _):
        st_copy(i).start()
        return 0

    lax.fori_loop(1, NY * NZ, st_start, 0)

    def st_wait(i, _):
        vv = rem(v + i, NY * NZ)
        remote(ST, SR.at[vv], st_send.at[0], st_recv.at[vv], g, v).wait_recv()
        return 0

    lax.fori_loop(1, NY * NZ, st_wait, 0)
    tops = SR[:, 0, :]
    top = jnp.max(tops, axis=0, keepdims=True)
    gap = tops - top
    fac = jnp.exp(gap)
    tot, m1, m2 = SR[:, 1, :], SR[:, 2, :], SR[:, 3, :]
    total = jnp.sum(fac * tot, axis=0, keepdims=True)
    mom1 = jnp.sum(fac * (m1 + gap * tot), axis=0, keepdims=True)
    mom2 = jnp.sum(fac * (m2 + 2.0 * gap * m1 + gap * gap * tot), axis=0, keepdims=True)
    val = jnp.sum(SR[:, 4, :], axis=0, keepdims=True)
    mean = mom1 / total
    var = mom2 / total - mean * mean
    score = (val - top - mean) / jnp.sqrt(jnp.maximum(var, 1.0))

    SS[...] = jnp.broadcast_to(score, (8, R))
    SC[g] = SS[...]

    def sc_copy(i):
        return remote(SS, SC.at[g], sc_send.at[i], sc_recv.at[g], rem(g + i, NX * NC), v)

    def sc_start(i, _):
        sc_copy(i).start()
        return 0

    lax.fori_loop(1, NX * NC, sc_start, 0)

    ends_of = jnp.broadcast_to(lengths[...], (8, 8))
    doc = lax.broadcasted_iota(I32, (8, 8), 0)
    at = lax.broadcasted_iota(I32, (8, 8), 1)
    ends = jnp.sum(jnp.where(at <= doc, ends_of, 0), axis=1, keepdims=True)
    starts = jnp.sum(jnp.where(at < doc, ends_of, 0), axis=1, keepdims=True)
    position = lax.broadcasted_iota(I32, (8, R), 1)
    member = (position >= starts) & (position < ends) & (flags[...] < NX * NC)
    sums = jnp.sum(jnp.where(member, SS[...], 0.0), axis=1, keepdims=True)
    counts = jnp.sum(jnp.where(member, 1.0, 0.0), axis=1, keepdims=True)
    means = sums / jnp.maximum(counts, 1.0)
    place = lax.broadcasted_iota(I32, (8, R), 0)
    result[:, R:] = jnp.sum(jnp.where(position == place, means, 0.0), axis=0, keepdims=True)

    def sc_wait(i, _):
        gg = rem(g + i, NX * NC)
        remote(SS, SC.at[gg], sc_send.at[0], sc_recv.at[gg], gg, v).wait_recv()
        return 0

    lax.fori_loop(1, NX * NC, sc_wait, 0)
    place = lax.broadcasted_iota(I32, (R, R), 0)
    spread = jnp.zeros((R, R), F32)
    for s in range(8):
        spread = spread + jnp.where(slots[s:s + 1, :] == place, SC[s, 0:1, :], 0.0)
    result[:, :R] = jnp.sum(jnp.transpose(spread), axis=0, keepdims=True)

    for i in range(1, 4):
        h_copy(i).wait_send()
        s1_copy(i).wait_send()

    @pl.when(plane != c)
    def _():
        s1_copy(0).wait_send()

    for k in range(4):
        @pl.when(rel < 4)
        def _(k=k):
            for cp in range(2):
                z_copy(k, 0, 0, cp, rel).wait_send()
                z_copy(k, 0, 1, cp, rel).wait_send()
        for t in range(1, 4):
            for way in range(2):
                j = origin(t, way)

                @pl.when(j < 4)
                def _(k=k, t=t, way=way, j=j):
                    for cp in range(2):
                        if t < reach[way][cp]:
                            z_copy(k, t, way, cp, j).wait_send()
        for cp in range(2):
            for j in range(4):
                y_copy(k, cp, j).wait_send()
        for n in range(NT):
            p_copy(k, n).wait_send()
        if k < 3:
            for hf in range(2):
                q_copy(k, hf).wait_send()

    def st_sent(i, _):
        st_copy(i).wait_send()
        return 0

    def sc_sent(i, _):
        f_copy(i).wait_send()
        sc_copy(i).wait_send()
        return 0

    lax.fori_loop(1, NY * NZ, st_sent, 0)
    lax.fori_loop(1, NX * NC, sc_sent, 0)


def shards(hidden, flags, targets, head, lengths):
    vmem = pl.BlockSpec(memory_space=pltpu.VMEM)
    anywhere = pl.BlockSpec(memory_space=pl.ANY)
    dma = pltpu.SemaphoreType.DMA
    out = pl.pallas_call(
        body,
        out_shape=jax.ShapeDtypeStruct((1, 2 * R), F32),
        in_specs=[anywhere, anywhere, vmem, vmem, vmem],
        out_specs=vmem,
        scratch_shapes=[
            pltpu.VMEM((8, R, KB), BF16),
            pltpu.VMEM((KB, VB), BF16),
            pltpu.VMEM((NY, R, HALF), BF16),
            pltpu.VMEM((4, 2, R, VB), F32),
            pltpu.VMEM((4, R, VB), F32),
            pltpu.VMEM((6, R, HV + EXT), I16),
            pltpu.VMEM((6, R, HV + EXT), I16),
            pltpu.VMEM((R, R), F32),
            pltpu.VMEM((8, R), F32),
            pltpu.VMEM((NY * NZ, 8, R), F32),
            pltpu.VMEM((8, R), I32),
            pltpu.VMEM((8, 8, R), I32),
            pltpu.VMEM((8, R), F32),
            pltpu.VMEM((8, 8, R), F32),
            pltpu.VMEM((8, R), I32),
            dma((4,)), dma((4,)), dma((4,)), dma((4,)), dma((8,)),
            dma((4, 4, 2, 2)), dma((4, 2, 4)),
            dma((4, 2, 4)), dma((4, 2, 4)),
            dma((4, NT)), dma((4, NT)),
            dma((6,)), dma((6,)),
            dma((32,)), dma((32,)),
            dma((8,)), dma((8,)), dma((8,)), dma((8,)),
        ],
        compiler_params=pltpu.CompilerParams(
            collective_id=0, has_side_effects=True, vmem_limit_bytes=60 * 1024 * 1024
        ),
        name="score",
    )(hidden, head, flags.reshape(1, R), targets.reshape(1, R), lengths)
    return out[0, :R], out[:, R:R + 8]


def solution(mesh):
    placed = (P("grp", "vocab"), P("grp", None), P("grp"), P("grp", "vocab"), P("grp", None))
    return jax.shard_map(
        shards, mesh=mesh, in_specs=placed, out_specs=(P("grp"), P("grp", None)), check_vma=False
    )
```

```python
import jax
import jax.numpy as jnp
from jax import lax
from jax.experimental import pallas as pl
from jax.experimental.pallas import tpu as pltpu
from jax.sharding import PartitionSpec as P

MESH = pl.DeviceIdType.MESH
F32, BF16, I32, I16 = jnp.float32, jnp.bfloat16, jnp.int32, jnp.int16

NX, NC, NY, NZ = 4, 2, 4, 8
R = 128
FEAT = 512
HALF = FEAT // 2
KB = 2048
VB = 2048
TN = 512
NT = VB // TN
CAP = 16
OFF = (2, 1, 3, 0)
CODE_MAX = 32767.0
UNIT = 0.4375
EXT = 128

HV = VB // 2

ORDER = sorted(((k, t) for k in range(4) for t in range(5)), key=lambda e: (3 * e[1] + 2 * e[0], e[0]))
EARLY = tuple(ORDER[:16])
LATE = {0: (ORDER[16],), 1: (ORDER[17],), 3: (ORDER[18],), 6: (ORDER[19],)}
POSTS = {3: ((0, 0),), 5: ((0, 1),), 7: ((1, 1),), 11: ((2, 0), (1, 0)), 13: ((2, 1),)}


def rem(a, n):
    return lax.rem(a, jnp.int32(n))


def div(a, n):
    return lax.div(a, jnp.int32(n))


def body(
    hidden, head, flags, targets, lengths, result,
    X, W, H, Pb, PR, Q, C, stats, ST, SR, FS, FB, SS, SC, slots,
    w_sem, h_send, h_recv, s1_send, s1_recv, z_send, z_recv, y_send, y_recv, p_send, p_recv,
    q_send, q_recv, st_send, st_recv, sc_send, sc_recv, f_send, f_recv,
):
    g = lax.axis_index("grp")
    v = lax.axis_index("vocab")
    x, c = div(g, NC), rem(g, NC)
    y, z = div(v, NZ), rem(v, NZ)
    rel = rem(z - 4 * c + NZ, NZ)
    h = rem(y, 2)
    plane = div(z, 4)

    def remote(src, dst, ss, rs, gg, vv):
        return pltpu.make_async_remote_copy(
            src_ref=src, dst_ref=dst, send_sem=ss, recv_sem=rs,
            device_id=(gg, vv), device_id_type=MESH,
        )

    def w_copy(j):
        return pltpu.make_async_copy(
            head.at[pl.ds(j * 512, 512)], W.at[pl.ds(j * 512, 512)], w_sem.at[j]
        )

    def half_of(side):
        return hidden.at[:, pl.ds(pl.multiple_of(side * HALF, HALF), HALF)]

    pltpu.make_async_copy(half_of(h), H.at[y], h_recv.at[y]).start()
    for j in range(4):
        w_copy(j).start()
    FS[...] = jnp.broadcast_to(flags[...], (8, R))

    barrier = pltpu.get_barrier_semaphore()

    def hello(gg, vv):
        pl.semaphore_signal(barrier, inc=1, device_id=(gg, vv), device_id_type=MESH)

    def hello_plane(i, _):
        hello(g, rem(v + i, NY * NZ))
        return 0

    def hello_grp(i, _):
        hello(rem(g + i, NX * NC), v)
        return 0

    lax.fori_loop(1, NX * NC, hello_grp, 0)

    lax.fori_loop(1, NY * NZ, hello_plane, 0)
    pl.semaphore_wait(barrier, NY * NZ - 1 + NX * NC - 1)

    j1 = rem(z, 4)

    def h_copy(i):
        yy = rem(y + i, NY)
        return remote(half_of(rem(yy, 2)), H.at[y], h_send.at[i], h_recv.at[y], g, yy * NZ + z)

    for i in (2, 1, 3):
        h_copy(i).start()

    def s1_owner(i):
        return rem(x + i, NX) * NC + plane

    def s1_refs(i):
        col = pl.multiple_of(j1 * FEAT + h * HALF, HALF)
        return H.at[rem(x + i, NX)], X.at[g, :, pl.ds(col, HALF)]

    def s1_copy(i):
        src, dst = s1_refs(i)
        return remote(src, dst, s1_send.at[i], s1_recv.at[g], s1_owner(i), v)

    for i in (2, 3, 1, 0):
        src, dst = s1_refs(i)
        pltpu.make_async_copy(src, src, h_recv.at[rem(x + i, NX)]).wait()
        if i:
            s1_copy(i).start()
            continue

        @pl.when(plane == c)
        def _(src=src, dst=dst):
            pltpu.make_async_copy(src, dst, s1_recv.at[g]).start()

        @pl.when(plane != c)
        def _():
            s1_copy(0).start()

    def f_copy(i):
        return remote(FS, FB.at[g], f_send.at[i], f_recv.at[g], rem(g + i, NX * NC), v)

    def f_start(i, _):
        f_copy(i).start()
        return 0

    lax.fori_loop(1, NX * NC, f_start, 0)
    FB[g] = FS[...]

    def chunk_at(k):
        return rem(x + OFF[k], NX)

    def unit(k, cp, j, hh):
        col = pl.multiple_of(j * FEAT + hh * HALF, HALF)
        return X.at[2 * chunk_at(k) + cp, :, pl.ds(col, HALF)]

    def z_copy(k, t, way, cp, j):
        ref = unit(k, cp, j, h)
        to = rem(z + (1 if way == 0 else NZ - 1), NZ)
        return remote(ref, ref, z_send.at[k, t, way, cp], z_recv.at[k, cp, j], g, y * NZ + to)

    def y_copy(k, cp, j):
        ref = unit(k, cp, j, h)
        to = rem(y + (1 if cp == 0 else NY - 1), NY)
        return remote(ref, ref, y_send.at[k, cp, j], y_recv.at[k, cp, j], g, to * NZ + z)

    reach = ((4, 3), (3, 4))

    def origin(t, way):
        return rem(rel + (NZ - t if way == 0 else t), NZ)

    def event(k, t):
        if t == 0:
            @pl.when(rel < 4)
            def _():
                for cp in range(2):
                    r = 2 * chunk_at(k) + cp
                    ref = unit(k, cp, rel, h)
                    pltpu.make_async_copy(ref, ref, s1_recv.at[r]).wait()
                    z_copy(k, 0, 0, cp, rel).start()
                    z_copy(k, 0, 1, cp, rel).start()
                    y_copy(k, cp, rel).start()
            return
        for way in range(2):
            j = origin(t, way)

            @pl.when(j < 4)
            def _(way=way, j=j):
                for cp in range(2):
                    if t > reach[way][cp]:
                        continue
                    ref = unit(k, cp, j, h)
                    remote(ref, ref, z_send.at[k, 0, way, cp], z_recv.at[k, cp, j], g, v).wait_recv()
                    if t < reach[way][cp]:
                        z_copy(k, t, way, cp, j).start()
                    y_copy(k, cp, j).start()

    for k, t in EARLY:
        event(k, t)
    for j in range(4):
        w_copy(j).wait()

    def p_copy(k, n):
        cols = pl.ds(pl.multiple_of(n * TN, TN), TN)
        return remote(
            Pb.at[k, 1 - c, :, cols], PR.at[k, :, cols],
            p_send.at[k, n], p_recv.at[k, n], x * NC + (1 - c), v,
        )

    def wait_y(k):
        for cp in range(2):
            for j in range(4):
                ref = unit(k, cp, j, 1 - h)
                remote(ref, ref, y_send.at[k, cp, j], y_recv.at[k, cp, j], g, v).wait_recv()

    right, left = rem(x + 1, NX) * NC + c, rem(x + NX - 1, NX) * NC + c

    def q_copy(k, hf):
        u = 2 * k + hf
        to = right if k == 1 or (k == 0 and hf == 0) else left
        return remote(Q.at[u], C.at[u], q_send.at[u], q_recv.at[u], to, v)

    def decode(u, rows):
        wide = C[u, rows, :].astype(I32).astype(F32)
        return wide[:, :HV] * (wide[:, HV:HV + 1] * (UNIT / CODE_MAX))

    def encode(total):
        top = jnp.max(jnp.abs(total), axis=1, keepdims=True)
        scale = jnp.maximum(jnp.ceil(top * (1.0 / UNIT)), 1.0)
        codes = jnp.round(total * (CODE_MAX / (scale * UNIT)))
        return (
            codes.astype(I32).astype(I16),
            jnp.broadcast_to(scale, (total.shape[0], EXT)).astype(I32).astype(I16),
        )

    def pair_sum(k, rows, hf):
        cols = slice(hf * HV, (hf + 1) * HV)
        return Pb[k, c, rows, cols] + PR[k, rows, cols]

    def wait_pair(k, hf):
        for n in (2 * hf, 2 * hf + 1):
            p_copy(k, n).wait_recv()

    def post(k, hf):
        wait_pair(k, hf)
        relayed = k == hf + 1
        if relayed:
            q_copy(0, hf).wait_recv()
        u = 2 * k + hf

        @pl.loop(0, R // 16)
        def _(i):
            rows = pl.ds(pl.multiple_of(i * 16, 16), 16)
            total = pair_sum(k, rows, hf)
            if relayed:
                total = total + decode(hf, rows)
            codes, scale = encode(total)
            Q[u, rows, :HV] = codes
            Q[u, rows, HV:] = scale

        q_copy(k, hf).start()

    def tile(step, _):
        k = div(step, NT)
        n = rem(step + jnp.where(k == 1, 2, 0), NT)
        for kk in range(4):
            @pl.when(step == kk * NT)
            def _(kk=kk):
                wait_y(kk)
        d = rem(x + jnp.where(k == 0, 2, jnp.where(k == 1, 1, jnp.where(k == 2, 3, 0))), NX)
        cols = pl.ds(pl.multiple_of(n * TN, TN), TN)
        rows = X[pl.ds(2 * d, 2)].reshape(2 * R, KB)
        out = jnp.dot(rows, W[:, cols], preferred_element_type=F32)
        Pb[k, :, :, cols] = out.reshape(2, R, TN)
        p_copy(k, n).start()
        for at, events in LATE.items():
            @pl.when(step == at)
            def _(events=events):
                for ev in events:
                    event(*ev)
        for at, blocks in POSTS.items():
            @pl.when(step == at)
            def _(blocks=blocks):
                for block in blocks:
                    post(*block)
        return 0

    lax.fori_loop(0, 4 * NT, tile, 0)

    def f_wait(i, _):
        gg = rem(g + i, NX * NC)
        remote(FS, FB.at[gg], f_send.at[0], f_recv.at[gg], gg, v).wait_recv()
        return 0

    lax.fori_loop(1, NX * NC, f_wait, 0)
    named = FB[:, 0, :] == g
    above = (
        lax.broadcasted_iota(I32, (R, R), 0) < lax.broadcasted_iota(I32, (R, R), 1)
    ).astype(BF16)
    rank = jnp.dot(named.astype(F32).astype(BF16), above, preferred_element_type=F32)
    shard = lax.broadcasted_iota(I32, (8, R), 0)
    slots[...] = jnp.where(named, shard * CAP + rank.astype(I32), -1)

    for hf in range(2):
        wait_pair(3, hf)
    want = jnp.transpose(jnp.broadcast_to(targets[...].astype(F32), (R, R)))
    stats[...] = want
    for hf in (1, 0):
        q_copy(1, hf).wait_recv()

        @pl.loop(0, R // 16)
        def _(i, hf=hf):
            rows = pl.ds(pl.multiple_of(i * 16, 16), 16)
            PR[3, rows, hf * HV:(hf + 1) * HV] = pair_sum(3, rows, hf) + decode(2 + hf, rows)

    for hf in range(2):
        q_copy(2, hf).wait_recv()

    @pl.loop(0, R // 16)
    def _(i):
        rows = pl.ds(pl.multiple_of(i * 16, 16), 16)
        logits = PR[3, rows, :] + jnp.concatenate([decode(4, rows), decode(5, rows)], axis=1)
        target = stats[rows, :][:, :1].astype(I32) - v * VB
        top = jnp.max(logits, axis=1, keepdims=True)
        shifted = logits - top
        scaled = jnp.exp(shifted)
        first = scaled * shifted
        total = jnp.sum(scaled, axis=1, keepdims=True)
        mom1 = jnp.sum(first, axis=1, keepdims=True)
        mom2 = jnp.sum(first * shifted, axis=1, keepdims=True)
        column = lax.broadcasted_iota(I32, (16, VB), 1)
        val = jnp.sum(jnp.where(column == target, logits, 0.0), axis=1, keepdims=True)
        lane = lax.broadcasted_iota(I32, (16, R), 1)
        stats[rows, :] = jnp.where(
            lane == 0, top,
            jnp.where(lane == 1, total, jnp.where(lane == 2, mom1, jnp.where(lane == 3, mom2, val))),
        )

    ST[...] = jnp.transpose(stats[...])[:8, :]
    SR[v] = ST[...]

    def st_copy(i):
        return remote(ST, SR.at[v], st_send.at[i], st_recv.at[v], g, rem(v + i, NY * NZ))

    def st_start(i, _):
        st_copy(i).start()
        return 0

    lax.fori_loop(1, NY * NZ, st_start, 0)

    def st_wait(i, _):
        vv = rem(v + i, NY * NZ)
        remote(ST, SR.at[vv], st_send.at[0], st_recv.at[vv], g, v).wait_recv()
        return 0

    lax.fori_loop(1, NY * NZ, st_wait, 0)
    tops = SR[:, 0, :]
    top = jnp.max(tops, axis=0, keepdims=True)
    gap = tops - top
    fac = jnp.exp(gap)
    tot, m1, m2 = SR[:, 1, :], SR[:, 2, :], SR[:, 3, :]
    total = jnp.sum(fac * tot, axis=0, keepdims=True)
    mom1 = jnp.sum(fac * (m1 + gap * tot), axis=0, keepdims=True)
    mom2 = jnp.sum(fac * (m2 + 2.0 * gap * m1 + gap * gap * tot), axis=0, keepdims=True)
    val = jnp.sum(SR[:, 4, :], axis=0, keepdims=True)
    mean = mom1 / total
    var = mom2 / total - mean * mean
    score = (val - top - mean) / jnp.sqrt(jnp.maximum(var, 1.0))

    SS[...] = jnp.broadcast_to(score, (8, R))
    SC[g] = SS[...]

    def sc_copy(i):
        return remote(SS, SC.at[g], sc_send.at[i], sc_recv.at[g], rem(g + i, NX * NC), v)

    def sc_start(i, _):
        sc_copy(i).start()
        return 0

    lax.fori_loop(1, NX * NC, sc_start, 0)

    ends_of = jnp.broadcast_to(lengths[...], (8, 8))
    doc = lax.broadcasted_iota(I32, (8, 8), 0)
    at = lax.broadcasted_iota(I32, (8, 8), 1)
    ends = jnp.sum(jnp.where(at <= doc, ends_of, 0), axis=1, keepdims=True)
    starts = jnp.sum(jnp.where(at < doc, ends_of, 0), axis=1, keepdims=True)
    position = lax.broadcasted_iota(I32, (8, R), 1)
    member = (position >= starts) & (position < ends) & (flags[...] < NX * NC)
    sums = jnp.sum(jnp.where(member, SS[...], 0.0), axis=1, keepdims=True)
    counts = jnp.sum(jnp.where(member, 1.0, 0.0), axis=1, keepdims=True)
    means = sums / jnp.maximum(counts, 1.0)
    place = lax.broadcasted_iota(I32, (8, R), 0)
    result[:, R:] = jnp.sum(jnp.where(position == place, means, 0.0), axis=0, keepdims=True)

    def sc_wait(i, _):
        gg = rem(g + i, NX * NC)
        remote(SS, SC.at[gg], sc_send.at[0], sc_recv.at[gg], gg, v).wait_recv()
        return 0

    lax.fori_loop(1, NX * NC, sc_wait, 0)
    place = lax.broadcasted_iota(I32, (R, R), 0)
    spread = jnp.zeros((R, R), F32)
    for s in range(8):
        spread = spread + jnp.where(slots[s:s + 1, :] == place, SC[s, 0:1, :], 0.0)
    result[:, :R] = jnp.sum(jnp.transpose(spread), axis=0, keepdims=True)

    for i in range(1, 4):
        h_copy(i).wait_send()
        s1_copy(i).wait_send()

    @pl.when(plane != c)
    def _():
        s1_copy(0).wait_send()

    for k in range(4):
        @pl.when(rel < 4)
        def _(k=k):
            for cp in range(2):
                z_copy(k, 0, 0, cp, rel).wait_send()
                z_copy(k, 0, 1, cp, rel).wait_send()
        for t in range(1, 4):
            for way in range(2):
                j = origin(t, way)

                @pl.when(j < 4)
                def _(k=k, t=t, way=way, j=j):
                    for cp in range(2):
                        if t < reach[way][cp]:
                            z_copy(k, t, way, cp, j).wait_send()
        for cp in range(2):
            for j in range(4):
                y_copy(k, cp, j).wait_send()
        for n in range(NT):
            p_copy(k, n).wait_send()
        if k < 3:
            for hf in range(2):
                q_copy(k, hf).wait_send()

    def st_sent(i, _):
        st_copy(i).wait_send()
        return 0

    def sc_sent(i, _):
        f_copy(i).wait_send()
        sc_copy(i).wait_send()
        return 0

    lax.fori_loop(1, NY * NZ, st_sent, 0)
    lax.fori_loop(1, NX * NC, sc_sent, 0)


def shards(hidden, flags, targets, head, lengths):
    vmem = pl.BlockSpec(memory_space=pltpu.VMEM)
    anywhere = pl.BlockSpec(memory_space=pl.ANY)
    dma = pltpu.SemaphoreType.DMA
    out = pl.pallas_call(
        body,
        out_shape=jax.ShapeDtypeStruct((1, 2 * R), F32),
        in_specs=[anywhere, anywhere, vmem, vmem, vmem],
        out_specs=vmem,
        scratch_shapes=[
            pltpu.VMEM((8, R, KB), BF16),
            pltpu.VMEM((KB, VB), BF16),
            pltpu.VMEM((NY, R, HALF), BF16),
            pltpu.VMEM((4, 2, R, VB), F32),
            pltpu.VMEM((4, R, VB), F32),
            pltpu.VMEM((6, R, HV + EXT), I16),
            pltpu.VMEM((6, R, HV + EXT), I16),
            pltpu.VMEM((R, R), F32),
            pltpu.VMEM((8, R), F32),
            pltpu.VMEM((NY * NZ, 8, R), F32),
            pltpu.VMEM((8, R), I32),
            pltpu.VMEM((8, 8, R), I32),
            pltpu.VMEM((8, R), F32),
            pltpu.VMEM((8, 8, R), F32),
            pltpu.VMEM((8, R), I32),
            dma((4,)), dma((4,)), dma((4,)), dma((4,)), dma((8,)),
            dma((4, 4, 2, 2)), dma((4, 2, 4)),
            dma((4, 2, 4)), dma((4, 2, 4)),
            dma((4, NT)), dma((4, NT)),
            dma((6,)), dma((6,)),
            dma((32,)), dma((32,)),
            dma((8,)), dma((8,)), dma((8,)), dma((8,)),
        ],
        compiler_params=pltpu.CompilerParams(
            collective_id=0, has_side_effects=True, vmem_limit_bytes=60 * 1024 * 1024
        ),
        name="score",
    )(hidden, head, flags.reshape(1, R), targets.reshape(1, R), lengths)
    return out[0, :R], out[:, R:R + 8]


def solution(mesh):
    placed = (P("grp", "vocab"), P("grp", None), P("grp"), P("grp", "vocab"), P("grp", None))
    return jax.shard_map(
        shards, mesh=mesh, in_specs=placed, out_specs=(P("grp"), P("grp", None)), check_vma=False
    )
```
